512 devices in a mesh: adv: 64 (over z, y_lo, core), imp: 8 (over x, y_hi).
Axes of the slice: x: 4, y: 4 (y_hi: 2, y_lo: 2; y = y_hi * 2 + y_lo), z: 16, core: 2. Of those that a mesh axis runs over, the one named last changes fastest.
Arguments:
- values: bfloat16 [16384, 16384], P('adv', 'imp'), may hold values from 0 to 4
- limits: float32 [16384], P('adv'), may hold values from 0.05 to 3
- start_pace: float32 [16384], P('adv'), may hold values from 0.3 to 1
- reserve: float32 [16384], P('imp'), may hold values from 0.2 to 1.2
Outputs:
- pace: float32 [16384], P('adv')
- prices: float32 [16384], P('imp')
The draws below stay inside these ranges and needn't reach their ends.
All inputs are finite; a program needn't handle non-finite values.
Results may differ from the reference program's by a relative error of at most 0.0003.
Values sent between devices are 32-bit elements; how exact they have to be, the bound alone decides.
No kernel may reach another device: no remote copies, remote signals or barrier semaphores. Data moves between devices by JAX's collectives and lax.ppermute only.
A program may use at most 64 MiB of HBM per device.

```python
import math
import jax
import jax.numpy as jnp
from jax import lax

M = 16384
ROUNDS = 2
A = 16384


def draw_values(key, part):
    first = jax.random.fold_in(jax.random.fold_in(key, 7), 0)
    column = 1.0 + 2.0 * jnp.arange(M, dtype=jnp.float32) / M
    base = jnp.exp(jax.random.uniform(first, (A, M), jnp.float32, -3.0, 0.0)) * column[None, :]
    return base.astype(jnp.bfloat16)


def level_of(key, dims, cuts, least, largest):
    loudness = 1.0
    for axis_at, blocks in cuts:
        draws = jax.random.uniform(jax.random.fold_in(jax.random.fold_in(key, 6), axis_at), (blocks,), jnp.float32, least / len(cuts), largest / len(cuts))
        loudness = loudness * jnp.repeat(jnp.exp(draws), dims[axis_at] // blocks).reshape((-1,) + (1,) * (len(dims) - 1 - axis_at))
    return loudness


def setup_inputs(seed: int = 0) -> dict:
    key_list = jax.random.split(jax.random.key(seed), 5)
    values = draw_values(jax.random.fold_in(key_list[4], 71), 0)
    limits = jnp.clip(jnp.exp(math.log(3.0) - 4.0943445 * jax.random.uniform(key_list[1], (A,), jnp.float32) ** level_of(key_list[1], (A,), ((0, 64),), -0.2, 0.2)), 0.05, 3.0)
    start_pace = jnp.clip(jnp.exp(math.log(1.0) - 1.2039728 * jax.random.uniform(key_list[2], (A,), jnp.float32) ** level_of(key_list[2], (A,), ((0, 64),), -0.2, 0.2)), 0.3, 1.0)
    reserve = jnp.clip(0.2 + 1 * jax.random.uniform(key_list[3], (M,), jnp.float32) ** level_of(key_list[3], (M,), ((0, 8),), -0.2, 0.2), 0.2, 1.2)
    return dict(values=values, limits=limits, start_pace=start_pace, reserve=reserve)


EPS = 0.015

def one_round(values, pace, limits, reserve):
    width = min(512, M)
    starts = (jnp.arange(M // width) * width).astype(jnp.int32)

    def block(spend, start):
        cols = lax.dynamic_slice_in_dim(values, start, width, 1).astype(jnp.float32)
        rlog = lax.dynamic_slice_in_dim(reserve, start, width, 0) / EPS
        bid = pace[:, None] * cols
        score = bid / EPS
        top = jnp.maximum(lax.optimization_barrier(jnp.max(score, axis=0)), rlog)
        total = lax.optimization_barrier(jnp.sum(jnp.exp(score - top[None, :]), axis=0)) + jnp.exp(rlog - top)
        lse = top + jnp.log(total)
        share = jnp.exp(score - lse[None, :])
        return (spend + lax.optimization_barrier(jnp.sum(share * bid, axis=1)), EPS * lse)
    spend, prices = lax.scan(block, jnp.zeros((values.shape[0],), jnp.float32), starts)
    new_pace = jnp.minimum(1.0, pace * jnp.sqrt(limits / spend))
    return (new_pace, prices.reshape(M))

def reference(values, limits, start_pace, reserve):
    pace = start_pace
    prices = jnp.zeros((M,), jnp.float32)
    for step in range(ROUNDS):
        pace, prices = one_round(values, pace, limits, reserve)
    return (pace, prices)
```

```python
import jax
import jax.numpy as jnp
from jax import lax
from jax.sharding import PartitionSpec as P

ROUNDS = 2


EPS = 0.015
NEAR = 4


def lse_of(x):
    top = jnp.max(x, axis=0)
    return top + jnp.log(jnp.sum(jnp.exp(x - top[None]), axis=0))


def on_device(far, near, groups_near, groups_far, values, limits, start_pace, reserve):
    pace = start_pace
    rlog = reserve / EPS
    prices = jnp.zeros_like(reserve)
    imp = lax.axis_size("imp")
    for step in range(ROUNDS):
        bid = pace[:, None] * values.astype(jnp.float32)
        score = bid / EPS
        own = lse_of(score)
        plane = lax.all_gather(own, "adv", axis_index_groups=groups_near)
        own = lse_of(plane)
        all_z = lax.all_to_all(
            jnp.broadcast_to(own, (far, own.shape[0])), "adv", 0, 0, axis_index_groups=groups_far, tiled=True
        )
        lse = lse_of(jnp.concatenate([all_z, rlog[None]], axis=0))
        prices = EPS * lse
        part = jnp.sum(jnp.exp(score - lse[None, :]) * bid, axis=1)
        parts = lax.all_to_all(jnp.broadcast_to(part, (imp, part.shape[0])), "imp", 0, 0, tiled=True)
        spend = jnp.sum(parts, axis=0)
        pace = jnp.minimum(1.0, pace * jnp.sqrt(limits / spend))
    return (pace, prices)


def solution(mesh):
    placed = (P("adv", "imp"), P("adv"), P("adv"), P("imp"))
    near = NEAR
    far = mesh.shape["adv"] // near
    groups_near = [[near * z + k for k in range(near)] for z in range(far)]
    groups_far = [[near * z + k for z in range(far)] for k in range(near)]

    def step(*args):
        return on_device(far, near, groups_near, groups_far, *args)

    return jax.shard_map(
        step, mesh=mesh, in_specs=placed, out_specs=(P("adv"), P("imp")), check_vma=False
    )
```

```python
import math

import jax
import jax.numpy as jnp
from jax import lax
from jax.experimental import pallas as pl
from jax.experimental.pallas import tpu as pltpu
from jax.sharding import PartitionSpec as P

EPS = 0.015
NEAR = 4
LANES = 128
CHUNKS = 4
UNIT = math.log2(math.e) / EPS
BACK = EPS / math.log2(math.e)
LOG2E = math.log2(math.e)

VMEM = pl.BlockSpec(memory_space=pltpu.VMEM)
HBM = pl.BlockSpec(memory_space=pltpu.HBM)


def log2(x):
    return jnp.log(x) * LOG2E


def spread_rows(scale_ref, pace, rows):
    for h in range(rows // LANES):
        row = jnp.broadcast_to(pace[h : h + 1, :] * UNIT, (LANES, LANES))
        scale_ref[pl.ds(h * LANES, LANES), :] = row.T


def strip_lse(s, v, scale_ref, lse_ref, top_ref, weighted_ref):
    y = v.astype(jnp.float32) * scale_ref[...]
    top = jnp.max(y, axis=0, keepdims=True)
    e = jnp.exp2(y - top)
    weighted_ref[:, pl.ds(s * LANES, LANES)] = y * e
    top_ref[pl.ds(s, 1), :] = top
    lse_ref[pl.ds(s, 1), :] = top + log2(jnp.sum(e, axis=0, keepdims=True))


def first_kernel(
    values_hbm, pace_hbm, limits_hbm, reserve_hbm,
    lse_ref, top_ref, weighted_ref, values_ref, pace_ref, limits_ref, reserve_ref,
    scale_ref, sems,
):
    rows, columns = values_ref.shape
    width = columns // CHUNKS
    small = []
    for n, (source, target) in enumerate(
        ((pace_hbm, pace_ref), (limits_hbm, limits_ref), (reserve_hbm, reserve_ref))
    ):
        small.append(pltpu.make_async_copy(source, target, sems.at[CHUNKS + n]))
    small[0].start()
    copies = []
    for c in range(CHUNKS):
        part = pl.ds(c * width, width)
        copies.append(pltpu.make_async_copy(values_hbm.at[:, part], values_ref.at[:, part], sems.at[c]))
        copies[c].start()
    small[1].start()
    small[2].start()
    small[0].wait()
    spread_rows(scale_ref, pace_ref[...], rows)
    per = width // LANES
    for c in range(CHUNKS):
        copies[c].wait()
        for s in range(c * per, (c + 1) * per):
            strip_lse(s, values_ref[:, pl.ds(s * LANES, LANES)], scale_ref, lse_ref, top_ref, weighted_ref)
    small[1].wait()
    small[2].wait()


def new_pace(parts, pace, limits):
    spend = jnp.sum(parts, axis=0) * BACK
    return jnp.minimum(1.0, pace * jnp.sqrt(limits / spend))


def next_kernel(values_ref, parts_ref, pace_ref, limits_ref, pace_out, lse_ref, top_ref, weighted_ref, scale_ref):
    rows, columns = values_ref.shape
    pace = new_pace(parts_ref[...], pace_ref[...], limits_ref[...])
    pace_out[...] = pace
    spread_rows(scale_ref, pace, rows)
    for s in range(columns // LANES):
        strip_lse(s, values_ref[:, pl.ds(s * LANES, LANES)], scale_ref, lse_ref, top_ref, weighted_ref)


def shares(z_ref, reserve_ref, top_ref, weighted_ref, parts_ref):
    rlog = reserve_ref[...] * UNIT
    peak = jnp.maximum(jnp.max(z_ref[...], axis=0), rlog)
    total = jnp.sum(jnp.exp2(z_ref[...] - peak[None]), axis=0) + jnp.exp2(rlog - peak)
    lse = peak + log2(total)
    w = jnp.exp2(top_ref[...] - lse)
    rows, columns = weighted_ref.shape
    acc = weighted_ref[:, pl.ds(0, LANES)] * w[0:1, :]
    for s in range(1, columns // LANES):
        acc = acc + weighted_ref[:, pl.ds(s * LANES, LANES)] * w[s : s + 1, :]
    for h in range(rows // LANES):
        part = jnp.sum(acc[h * LANES : (h + 1) * LANES, :].T, axis=0, keepdims=True)
        parts_ref[:, pl.ds(h, 1), :] = jnp.broadcast_to(part[None], (parts_ref.shape[0], 1, LANES))
    return lse


def spend_kernel(z_ref, reserve_ref, top_ref, weighted_ref, parts_ref):
    shares(z_ref, reserve_ref, top_ref, weighted_ref, parts_ref)


def last_spend_kernel(z_ref, reserve_ref, top_ref, weighted_ref, parts_ref, prices_ref):
    prices_ref[...] = BACK * shares(z_ref, reserve_ref, top_ref, weighted_ref, parts_ref)


PARAMS = pltpu.CompilerParams(vmem_limit_bytes=16 * 2**20)


def f32(*shape):
    return jax.ShapeDtypeStruct(shape, jnp.float32)


def on_device(far, near, groups_near, groups_far, values, limits, start_pace, reserve):
    rows, columns = values.shape
    imp = lax.axis_size("imp")
    strips, halves = columns // LANES, rows // LANES
    limits = limits.reshape(halves, LANES)
    pace = start_pace.reshape(halves, LANES)
    reserve = reserve.reshape(strips, LANES)
    row_lse = (f32(strips, LANES), f32(strips, LANES), f32(rows, columns))

    def to_all_z(own):
        plane = lax.all_gather(own, "adv", axis_index_groups=groups_near)
        peak = jnp.max(plane, axis=0)
        own = peak + log2(jnp.sum(jnp.exp2(plane - peak[None]), axis=0))
        return lax.all_to_all(
            jnp.broadcast_to(own[None], (far, strips, LANES)), "adv", 0, 0, axis_index_groups=groups_far, tiled=True
        )

    own, top, weighted, values, pace, limits, reserve = pl.pallas_call(
        first_kernel,
        compiler_params=PARAMS,
        out_shape=row_lse
        + (jax.ShapeDtypeStruct((rows, columns), values.dtype), f32(halves, LANES), f32(halves, LANES), f32(strips, LANES)),
        in_specs=[HBM] * 4,
        out_specs=(VMEM,) * 7,
        scratch_shapes=[
            pltpu.VMEM((rows, LANES), jnp.float32),
            pltpu.SemaphoreType.DMA((CHUNKS + 3,)),
        ],
    )(*(pltpu.with_memory_space_constraint(a, pltpu.HBM) for a in (values, pace, limits, reserve)))
    parts = pl.pallas_call(
        spend_kernel,
        compiler_params=PARAMS,
        out_shape=f32(imp, halves, LANES),
        in_specs=[VMEM] * 4,
        out_specs=VMEM,
    )(to_all_z(own), reserve, top, weighted)
    parts = lax.all_to_all(parts, "imp", 0, 0, tiled=True)
    pace, own, top, weighted = pl.pallas_call(
        next_kernel,
        compiler_params=PARAMS,
        out_shape=(f32(halves, LANES),) + row_lse,
        in_specs=[VMEM] * 4,
        out_specs=(VMEM,) * 4,
        scratch_shapes=[pltpu.VMEM((rows, LANES), jnp.float32)],
    )(values, parts, pace, limits)
    parts, prices = pl.pallas_call(
        last_spend_kernel,
        compiler_params=PARAMS,
        out_shape=(f32(imp, halves, LANES), f32(strips, LANES)),
        in_specs=[VMEM] * 4,
        out_specs=(VMEM, VMEM),
    )(to_all_z(own), reserve, top, weighted)
    parts = lax.all_to_all(parts, "imp", 0, 0, tiled=True)
    pace = new_pace(parts, pace, limits)
    return (pace.reshape(rows), prices.reshape(columns))


def solution(mesh):
    placed = (P("adv", "imp"), P("adv"), P("adv"), P("imp"))
    near = NEAR
    far = mesh.shape["adv"] // near
    groups_near = [[near * z + k for k in range(near)] for z in range(far)]
    groups_far = [[near * z + k for z in range(far)] for k in range(near)]

    def step(*args):
        return on_device(far, near, groups_near, groups_far, *args)

    return jax.shard_map(
        step, mesh=mesh, in_specs=placed, out_specs=(P("adv"), P("imp")), check_vma=False
    )
```

```python
import math

import jax
import jax.numpy as jnp
from jax import lax
from jax.experimental import pallas as pl
from jax.experimental.pallas import tpu as pltpu
from jax.sharding import PartitionSpec as P

EPS = 0.015
CORES = 2
NEAR = 4
LANES = 128
CHUNKS = 4
UNIT = math.log2(math.e) / EPS
BACK = EPS / math.log2(math.e)
LOG2E = math.log2(math.e)

VMEM = pl.BlockSpec(memory_space=pltpu.VMEM)
HBM = pl.BlockSpec(memory_space=pltpu.HBM)
PARAMS = pltpu.CompilerParams(vmem_limit_bytes=16 * 2**20)


def log2(x):
    return jnp.log(x) * LOG2E


def join(x):
    peak = jnp.max(x, axis=0)
    return peak + log2(jnp.sum(jnp.exp2(x - peak[None]), axis=0))


def join_kernel(x_ref, out_ref):
    strips = out_ref.shape[-2]
    out_ref[...] = jnp.broadcast_to(join(x_ref[:, pl.ds(0, strips), :]), out_ref.shape)


def joined(x, *shape):
    return pl.pallas_call(
        join_kernel,
        compiler_params=PARAMS,
        out_shape=jax.ShapeDtypeStruct(shape, jnp.float32),
        in_specs=[VMEM],
        out_specs=VMEM,
    )(x)


def strip(s):
    return pl.ds(s * LANES, LANES)


def spread_rows(scale_ref, pace):
    for h in range(scale_ref.shape[0] // LANES):
        row = jnp.broadcast_to(pace[h : h + 1, :] * UNIT, (LANES, LANES))
        scale_ref[strip(h), :] = row.T


def strip_lse(s, v, scale_ref, weighted_ref):
    y = v.astype(jnp.float32) * scale_ref[...]
    top = jnp.max(y, axis=0, keepdims=True)
    e = jnp.exp2(y - top)
    weighted_ref[:, strip(s)] = y * e
    return top, top + log2(jnp.sum(e, axis=0, keepdims=True))


def first_kernel(
    values_hbm, pace_hbm, limits_hbm, reserve_hbm,
    send_ref, top_ref, weighted_ref, values_ref, wide_ref, reserve_ref,
    pace_ref, limits_ref, scale_ref, sems,
):
    rows, columns = values_ref.shape
    strips, halves = columns // LANES, rows // LANES
    width = columns // CHUNKS
    pairs = ((pace_hbm, pace_ref), (limits_hbm, limits_ref), (reserve_hbm, reserve_ref))
    small = [pltpu.make_async_copy(a, b, sems.at[CHUNKS + n]) for n, (a, b) in enumerate(pairs)]
    small[0].start()
    copies = []
    for c in range(CHUNKS):
        part = pl.ds(c * width, width)
        copies.append(pltpu.make_async_copy(values_hbm.at[:, part], values_ref.at[:, part], sems.at[c]))
        copies[c].start()
    small[1].start()
    small[2].start()
    small[0].wait()
    send_ref[pl.ds(strips, halves), :] = pace_ref[...]
    spread_rows(scale_ref, pace_ref[...])
    per = width // LANES
    for c in range(CHUNKS):
        copies[c].wait()
        for s in range(c * per, (c + 1) * per):
            v = values_ref[:, strip(s)].astype(jnp.float32)
            wide_ref[:, strip(s)] = v
            top, lse = strip_lse(s, v, scale_ref, weighted_ref)
            top_ref[pl.ds(s, 1), :] = top
            send_ref[pl.ds(s, 1), :] = lse
    small[1].wait()
    send_ref[pl.ds(strips + halves, halves), :] = limits_ref[...]
    send_ref[pl.ds(strips + 2 * halves, 4), :] = jnp.zeros((4, LANES), jnp.float32)
    small[2].wait()


def new_pace(parts, pace, limits):
    spend = jnp.sum(parts, axis=0) * BACK
    return jnp.minimum(1.0, pace * jnp.sqrt(limits / spend))


def next_kernel(
    values_ref, other_ref, parts_ref, send_ref, pair_ref,
    pace_out, limits_out, lse_ref, top_ref, weighted_ref, scale_ref,
):
    rows, columns = values_ref.shape
    strips, halves = columns // LANES, rows // LANES
    both = 2 * halves
    mine = send_ref[pl.ds(strips, both), :]
    theirs = pair_ref[0, pl.ds(strips, both), :]
    pace = jnp.concatenate([mine[:halves], theirs[:halves]], axis=0)
    limits = jnp.concatenate([mine[halves:], theirs[halves:]], axis=0)
    pace = new_pace(parts_ref[...], pace, limits)
    pace_out[...] = pace
    limits_out[...] = limits
    ends = []
    for k, source in enumerate((values_ref, other_ref)):
        block = pl.ds(k * rows, rows)
        spread_rows(scale_ref.at[block], pace[k * halves : (k + 1) * halves])
    for s in range(strips):
        for k, source in enumerate((values_ref, other_ref)):
            block = pl.ds(k * rows, rows)
            top, lse = strip_lse(s, source[:, strip(s)], scale_ref.at[block], weighted_ref.at[block])
            top_ref[k, pl.ds(s, 1), :] = top
            ends.append(lse)
        one, two = ends[-2:]
        peak = jnp.maximum(one, two)
        lse_ref[pl.ds(s, 1), :] = peak + log2(jnp.exp2(one - peak) + jnp.exp2(two - peak))


def total_lse(z_ref, reserve_ref):
    rlog = reserve_ref[...] * UNIT
    peak = jnp.maximum(jnp.max(z_ref[...], axis=0), rlog)
    total = jnp.sum(jnp.exp2(z_ref[...] - peak[None]), axis=0) + jnp.exp2(rlog - peak)
    return peak + log2(total)


def put_parts(parts_ref, first, acc):
    for h in range(acc.shape[0] // LANES):
        part = jnp.sum(acc[h * LANES : (h + 1) * LANES, :].T, axis=0, keepdims=True)
        parts_ref[:, pl.ds(first + h, 1), :] = jnp.broadcast_to(part[None], (parts_ref.shape[0], 1, LANES))


def weighted_sums(weighted_ref, block, w):
    acc = weighted_ref[block, strip(0)] * w[0:1, :]
    for s in range(1, w.shape[0]):
        acc = acc + weighted_ref[block, strip(s)] * w[s : s + 1, :]
    return acc


def spend_kernel(z_ref, reserve_ref, top_ref, weighted_ref, other_ref, pair_ref, parts_ref, scale_ref):
    rows, columns = weighted_ref.shape
    strips, halves = columns // LANES, rows // LANES
    lse = total_lse(z_ref, reserve_ref)
    spread_rows(scale_ref, pair_ref[0, pl.ds(strips, halves), :])
    put_parts(parts_ref, 0, weighted_sums(weighted_ref, pl.ds(0, rows), jnp.exp2(top_ref[...] - lse)))
    for h in range(halves):
        acc = jnp.zeros((LANES, LANES), jnp.float32)
        for s in range(strips):
            y = other_ref[strip(h), strip(s)] * scale_ref[strip(h), :]
            acc = acc + y * jnp.exp2(y - lse[s : s + 1, :])
        put_parts(parts_ref, halves + h, acc)


def last_spend_kernel(z_ref, reserve_ref, top_ref, weighted_ref, parts_ref, prices_ref):
    rows = weighted_ref.shape[0] // 2
    lse = total_lse(z_ref, reserve_ref)
    prices_ref[...] = BACK * lse
    for k in range(2):
        w = jnp.exp2(top_ref[k] - lse)
        put_parts(parts_ref, k * (rows // LANES), weighted_sums(weighted_ref, pl.ds(k * rows, rows), w))


def f32(*shape):
    return jax.ShapeDtypeStruct(shape, jnp.float32)


def on_device(groups, values, limits, start_pace, reserve):
    rows, columns = values.shape
    imp = lax.axis_size("imp")
    far = lax.axis_size("adv") // NEAR
    strips, halves = columns // LANES, rows // LANES
    both = 2 * halves
    args = (values, start_pace.reshape(halves, LANES), limits.reshape(halves, LANES), reserve.reshape(strips, LANES))
    args = [pltpu.with_memory_space_constraint(a, pltpu.HBM) for a in args]

    def along_z(own):
        own = joined(lax.all_gather(own, "adv", axis_index_groups=groups["chips"]), far, strips, LANES)
        return lax.all_to_all(own, ("adv", "imp"), 0, 0, axis_index_groups=groups["z"], tiled=True)

    send, top, weighted, values, wide, reserve = pl.pallas_call(
        first_kernel,
        compiler_params=PARAMS,
        out_shape=(
            f32(strips + 2 * halves + 4, LANES),
            f32(strips, LANES),
            f32(rows, columns),
            jax.ShapeDtypeStruct((rows, columns), values.dtype),
            f32(rows, columns),
            f32(strips, LANES),
        ),
        in_specs=[HBM] * 4,
        out_specs=(VMEM,) * 6,
        scratch_shapes=[
            pltpu.VMEM((halves, LANES), jnp.float32),
            pltpu.VMEM((halves, LANES), jnp.float32),
            pltpu.VMEM((rows, LANES), jnp.float32),
            pltpu.SemaphoreType.DMA((CHUNKS + 3,)),
        ],
    )(*args)
    pair = lax.all_gather(send, "adv", axis_index_groups=groups["cores"])
    wide, pair = lax.optimization_barrier((wide, pair))
    other = lax.ppermute(wide, "adv", groups["ship"])
    parts = pl.pallas_call(
        spend_kernel,
        compiler_params=PARAMS,
        out_shape=f32(imp, both, LANES),
        in_specs=[VMEM] * 6,
        out_specs=VMEM,
        scratch_shapes=[pltpu.VMEM((rows, LANES), jnp.float32)],
    )(along_z(joined(pair, strips, LANES)), reserve, top, weighted, other, pair)
    parts = lax.all_to_all(parts, "imp", 0, 0, tiled=True)
    pace, limits, own, top, weighted = pl.pallas_call(
        next_kernel,
        compiler_params=PARAMS,
        out_shape=(
            f32(both, LANES),
            f32(both, LANES),
            f32(strips, LANES),
            f32(2, strips, LANES),
            f32(2 * rows, columns),
        ),
        in_specs=[VMEM] * 5,
        out_specs=(VMEM,) * 5,
        scratch_shapes=[pltpu.VMEM((2 * rows, LANES), jnp.float32)],
    )(values, other, parts, send, pair)
    parts, prices = pl.pallas_call(
        last_spend_kernel,
        compiler_params=PARAMS,
        out_shape=(f32(imp, both, LANES), f32(strips, LANES)),
        in_specs=[VMEM] * 4,
        out_specs=(VMEM, VMEM),
    )(along_z(own), reserve, top, weighted)
    parts = lax.all_to_all(parts, "imp", 0, 0, tiled=True)
    pace = new_pace(parts, pace, limits)
    done = jnp.concatenate([prices, pace, jnp.zeros((8 - both, LANES), jnp.float32)], axis=0)
    done = lax.all_gather(done, "adv", axis_index_groups=groups["cores"])[1]
    mine = done[strips : strips + halves]
    theirs = done[strips + halves : strips + both]
    pace = jnp.where(lax.axis_index("adv") % CORES == 1, mine, theirs)
    return (pace.reshape(rows), done[:strips].reshape(columns))


def solution(mesh):
    placed = (P("adv", "imp"), P("adv"), P("adv"), P("imp"))
    adv, imp = mesh.shape["adv"], mesh.shape["imp"]
    far, chips = adv // NEAR, NEAR // CORES

    def at(z, chip, core):
        return z * NEAR + chip * CORES + core

    along_z = [[at(z, c, 1) * imp + i for z in range(far)] for c in range(chips) for i in range(imp)]
    plane = [at(z, c, 0) * imp + i for z in range(far) for c in range(chips) for i in range(imp)]
    groups = dict(
        cores=[[at(z, c, k) for k in range(CORES)] for z in range(far) for c in range(chips)],
        chips=[[at(z, c, k) for c in range(chips)] for z in range(far) for k in range(CORES)],
        ship=[(at(z, c, 0), at(z, c, 1)) for z in range(far) for c in range(chips)],
        z=along_z + [plane[n : n + far] for n in range(0, len(plane), far)],
    )

    def step(*args):
        return on_device(groups, *args)

    return jax.shard_map(
        step, mesh=mesh, in_specs=placed, out_specs=(P("adv"), P("imp")), check_vma=False
    )
```

```python
import math

import jax
import jax.numpy as jnp
from jax import lax
from jax.experimental import pallas as pl
from jax.experimental.pallas import tpu as pltpu
from jax.sharding import PartitionSpec as P

EPS = 0.015
CORES = 2
NEAR = 4
LANES = 128
CHUNKS = 4
UNIT = math.log2(math.e) / EPS
BACK = EPS / math.log2(math.e)
LOG2E = math.log2(math.e)

VMEM = pl.BlockSpec(memory_space=pltpu.VMEM)
HBM = pl.BlockSpec(memory_space=pltpu.HBM)
PARAMS = pltpu.CompilerParams(vmem_limit_bytes=16 * 2**20)


def log2(x):
    return jnp.log(x) * LOG2E


def join(x):
    peak = jnp.max(x, axis=0)
    return peak + log2(jnp.sum(jnp.exp2(x - peak[None]), axis=0))


def join_kernel(x_ref, out_ref):
    strips = out_ref.shape[-2]
    out_ref[...] = jnp.broadcast_to(join(x_ref[:, pl.ds(0, strips), :]), out_ref.shape)


def joined(x, *shape):
    return pl.pallas_call(
        join_kernel,
        compiler_params=PARAMS,
        out_shape=jax.ShapeDtypeStruct(shape, jnp.float32),
        in_specs=[VMEM],
        out_specs=VMEM,
    )(x)


def strip(s):
    return pl.ds(s * LANES, LANES)


def spread_rows(scale_ref, pace):
    for h in range(scale_ref.shape[0] // LANES):
        row = jnp.broadcast_to(pace[h : h + 1, :] * UNIT, (LANES, LANES))
        scale_ref[strip(h), :] = row.T


def strip_lse(s, v, scale_ref, weighted_ref):
    y = v.astype(jnp.float32) * scale_ref[...]
    top = jnp.max(y, axis=0, keepdims=True)
    e = jnp.exp2(y - top)
    weighted_ref[:, strip(s)] = y * e
    return top, top + log2(jnp.sum(e, axis=0, keepdims=True))


def first_kernel(
    values_hbm, pace_hbm, limits_hbm, reserve_hbm,
    send_ref, top_ref, weighted_ref, values_ref, wide_ref, reserve_ref,
    pace_ref, limits_ref, scale_ref, sems,
):
    rows, columns = values_ref.shape
    strips, halves = columns // LANES, rows // LANES
    width = columns // CHUNKS
    pairs = ((pace_hbm, pace_ref), (limits_hbm, limits_ref), (reserve_hbm, reserve_ref))
    small = [pltpu.make_async_copy(a, b, sems.at[CHUNKS + n]) for n, (a, b) in enumerate(pairs)]
    small[0].start()
    copies = []
    for c in range(CHUNKS):
        part = pl.ds(c * width, width)
        copies.append(pltpu.make_async_copy(values_hbm.at[:, part], values_ref.at[:, part], sems.at[c]))
        copies[c].start()
    small[1].start()
    small[2].start()
    small[0].wait()
    send_ref[pl.ds(strips, halves), :] = pace_ref[...]
    spread_rows(scale_ref, pace_ref[...])
    per = width // LANES
    for c in range(CHUNKS):
        copies[c].wait()
        for s in range(c * per, (c + 1) * per):
            v = values_ref[:, strip(s)].astype(jnp.float32)
            wide_ref[:, strip(s)] = v
            top, lse = strip_lse(s, v, scale_ref, weighted_ref)
            top_ref[pl.ds(s, 1), :] = top
            send_ref[pl.ds(s, 1), :] = lse
    small[1].wait()
    send_ref[pl.ds(strips + halves, halves), :] = limits_ref[...]
    send_ref[pl.ds(strips + 2 * halves, 4), :] = jnp.zeros((4, LANES), jnp.float32)
    small[2].wait()


def new_pace(parts, pace, limits):
    spend = jnp.sum(parts, axis=0) * BACK
    return jnp.minimum(1.0, pace * jnp.sqrt(limits / spend))


def next_kernel(
    values_ref, other_ref, parts_ref, send_ref, pair_ref,
    pace_out, limits_out, lse_ref, top_ref, weighted_ref, scale_ref,
):
    rows, columns = values_ref.shape
    strips, halves = columns // LANES, rows // LANES
    both = 2 * halves
    mine = send_ref[pl.ds(strips, both), :]
    theirs = pair_ref[0, pl.ds(strips, both), :]
    pace = jnp.concatenate([mine[:halves], theirs[:halves]], axis=0)
    limits = jnp.concatenate([mine[halves:], theirs[halves:]], axis=0)
    pace = new_pace(parts_ref[...], pace, limits)
    pace_out[...] = pace
    limits_out[...] = limits
    ends = []
    for k, source in enumerate((values_ref, other_ref)):
        block = pl.ds(k * rows, rows)
        spread_rows(scale_ref.at[block], pace[k * halves : (k + 1) * halves])
    for s in range(strips):
        for k, source in enumerate((values_ref, other_ref)):
            block = pl.ds(k * rows, rows)
            top, lse = strip_lse(s, source[:, strip(s)], scale_ref.at[block], weighted_ref.at[block])
            top_ref[k, pl.ds(s, 1), :] = top
            ends.append(lse)
        one, two = ends[-2:]
        peak = jnp.maximum(one, two)
        lse_ref[pl.ds(s, 1), :] = peak + log2(jnp.exp2(one - peak) + jnp.exp2(two - peak))


def total_lse(z_ref, reserve_ref):
    rlog = reserve_ref[...] * UNIT
    peak = jnp.maximum(jnp.max(z_ref[...], axis=0), rlog)
    total = jnp.sum(jnp.exp2(z_ref[...] - peak[None]), axis=0) + jnp.exp2(rlog - peak)
    return peak + log2(total)


def put_parts(parts_ref, first, acc):
    for h in range(acc.shape[0] // LANES):
        part = jnp.sum(acc[h * LANES : (h + 1) * LANES, :].T, axis=0, keepdims=True)
        parts_ref[:, pl.ds(first + h, 1), :] = jnp.broadcast_to(part[None], (parts_ref.shape[0], 1, LANES))


def weighted_sums(weighted_ref, block, w):
    acc = weighted_ref[block, strip(0)] * w[0:1, :]
    for s in range(1, w.shape[0]):
        acc = acc + weighted_ref[block, strip(s)] * w[s : s + 1, :]
    return acc


def spend_kernel(z_ref, reserve_ref, top_ref, weighted_ref, other_ref, pair_ref, parts_ref, scale_ref):
    rows, columns = weighted_ref.shape
    strips, halves = columns // LANES, rows // LANES
    lse = total_lse(z_ref, reserve_ref)
    spread_rows(scale_ref, pair_ref[0, pl.ds(strips, halves), :])
    put_parts(parts_ref, 0, weighted_sums(weighted_ref, pl.ds(0, rows), jnp.exp2(top_ref[...] - lse)))
    for h in range(halves):
        acc = jnp.zeros((LANES, LANES), jnp.float32)
        for s in range(strips):
            y = other_ref[strip(h), strip(s)] * scale_ref[strip(h), :]
            acc = acc + y * jnp.exp2(y - lse[s : s + 1, :])
        put_parts(parts_ref, halves + h, acc)


def last_spend_kernel(z_ref, reserve_ref, top_ref, weighted_ref, parts_ref, prices_ref):
    rows = weighted_ref.shape[0] // 2
    lse = total_lse(z_ref, reserve_ref)
    prices_ref[...] = BACK * lse
    for k in range(2):
        w = jnp.exp2(top_ref[k] - lse)
        put_parts(parts_ref, k * (rows // LANES), weighted_sums(weighted_ref, pl.ds(k * rows, rows), w))


def pack_kernel(parts_ref, pace_ref, limits_ref, prices_ref, out_ref):
    strips, both = prices_ref.shape[0], pace_ref.shape[0]
    out_ref[pl.ds(0, strips), :] = prices_ref[...]
    out_ref[pl.ds(strips, both), :] = new_pace(parts_ref[...], pace_ref[...], limits_ref[...])
    out_ref[pl.ds(strips + both, 8 - both), :] = jnp.zeros((8 - both, LANES), jnp.float32)


def pick_kernel(pair_ref, pace_ref, prices_ref):
    strips, halves = prices_ref.shape[0], pace_ref.shape[0]
    prices_ref[...] = pair_ref[1, pl.ds(0, strips), :]
    second = lax.axis_index("adv") % CORES == 1
    mine = pair_ref[1, pl.ds(strips, halves), :]
    theirs = pair_ref[1, pl.ds(strips + halves, halves), :]
    pace_ref[...] = jnp.where(second, mine, theirs)


def f32(*shape):
    return jax.ShapeDtypeStruct(shape, jnp.float32)


def on_device(groups, values, limits, start_pace, reserve):
    rows, columns = values.shape
    imp = lax.axis_size("imp")
    far = lax.axis_size("adv") // NEAR
    strips, halves = columns // LANES, rows // LANES
    both = 2 * halves
    args = (values, start_pace.reshape(halves, LANES), limits.reshape(halves, LANES), reserve.reshape(strips, LANES))
    args = [pltpu.with_memory_space_constraint(a, pltpu.HBM) for a in args]

    def along_z(own):
        own = joined(lax.all_gather(own, "adv", axis_index_groups=groups["chips"]), far, strips, LANES)
        return lax.all_to_all(own, ("adv", "imp"), 0, 0, axis_index_groups=groups["z"], tiled=True)

    send, top, weighted, values, wide, reserve = pl.pallas_call(
        first_kernel,
        compiler_params=PARAMS,
        out_shape=(
            f32(strips + 2 * halves + 4, LANES),
            f32(strips, LANES),
            f32(rows, columns),
            jax.ShapeDtypeStruct((rows, columns), values.dtype),
            f32(rows, columns),
            f32(strips, LANES),
        ),
        in_specs=[HBM] * 4,
        out_specs=(VMEM,) * 6,
        scratch_shapes=[
            pltpu.VMEM((halves, LANES), jnp.float32),
            pltpu.VMEM((halves, LANES), jnp.float32),
            pltpu.VMEM((rows, LANES), jnp.float32),
            pltpu.SemaphoreType.DMA((CHUNKS + 3,)),
        ],
    )(*args)
    pair = lax.all_gather(send, "adv", axis_index_groups=groups["cores"])
    wide, pair = lax.optimization_barrier((wide, pair))
    other = lax.ppermute(wide, "adv", groups["ship"])
    parts = pl.pallas_call(
        spend_kernel,
        compiler_params=PARAMS,
        out_shape=f32(imp, both, LANES),
        in_specs=[VMEM] * 6,
        out_specs=VMEM,
        scratch_shapes=[pltpu.VMEM((rows, LANES), jnp.float32)],
    )(along_z(joined(pair, strips, LANES)), reserve, top, weighted, other, pair)
    parts = lax.all_to_all(parts, "imp", 0, 0, tiled=True)
    pace, limits, own, top, weighted = pl.pallas_call(
        next_kernel,
        compiler_params=PARAMS,
        out_shape=(
            f32(both, LANES),
            f32(both, LANES),
            f32(strips, LANES),
            f32(2, strips, LANES),
            f32(2 * rows, columns),
        ),
        in_specs=[VMEM] * 5,
        out_specs=(VMEM,) * 5,
        scratch_shapes=[pltpu.VMEM((2 * rows, LANES), jnp.float32)],
    )(values, other, parts, send, pair)
    parts, prices = pl.pallas_call(
        last_spend_kernel,
        compiler_params=PARAMS,
        out_shape=(f32(imp, both, LANES), f32(strips, LANES)),
        in_specs=[VMEM] * 4,
        out_specs=(VMEM, VMEM),
    )(along_z(own), reserve, top, weighted)
    parts = lax.all_to_all(parts, "imp", 0, 0, tiled=True)
    done = pl.pallas_call(
        pack_kernel,
        compiler_params=PARAMS,
        out_shape=f32(strips + 8, LANES),
        in_specs=[VMEM] * 4,
        out_specs=VMEM,
    )(parts, pace, limits, prices)
    pace, prices = pl.pallas_call(
        pick_kernel,
        compiler_params=PARAMS,
        out_shape=(f32(halves, LANES), f32(strips, LANES)),
        in_specs=[VMEM],
        out_specs=(VMEM, VMEM),
    )(lax.all_gather(done, "adv", axis_index_groups=groups["cores"]))
    return (pace.reshape(rows), prices.reshape(columns))


def solution(mesh):
    placed = (P("adv", "imp"), P("adv"), P("adv"), P("imp"))
    adv, imp = mesh.shape["adv"], mesh.shape["imp"]
    far, chips = adv // NEAR, NEAR // CORES

    def at(z, chip, core):
        return z * NEAR + chip * CORES + core

    along_z = [[at(z, c, 1) * imp + i for z in range(far)] for c in range(chips) for i in range(imp)]
    plane = [at(z, c, 0) * imp + i for z in range(far) for c in range(chips) for i in range(imp)]
    groups = dict(
        cores=[[at(z, c, k) for k in range(CORES)] for z in range(far) for c in range(chips)],
        chips=[[at(z, c, k) for c in range(chips)] for z in range(far) for k in range(CORES)],
        ship=[(at(z, c, 0), at(z, c, 1)) for z in range(far) for c in range(chips)],
        z=along_z + [plane[n : n + far] for n in range(0, len(plane), far)],
    )

    def step(*args):
        return on_device(groups, *args)

    return jax.shard_map(
        step, mesh=mesh, in_specs=placed, out_specs=(P("adv"), P("imp")), check_vma=False
    )
```

```python
import math

import jax
import jax.numpy as jnp
from jax import lax
from jax.experimental import pallas as pl
from jax.experimental.pallas import tpu as pltpu
from jax.sharding import PartitionSpec as P

EPS = 0.015
CORES = 2
NEAR = 4
LANES = 128
CHUNKS = 4
FIRST_Z = 9
FIRST_IMP = 5
UNIT = math.log2(math.e) / EPS
BACK = EPS / math.log2(math.e)
LOG2E = math.log2(math.e)

VMEM = pl.BlockSpec(memory_space=pltpu.VMEM)
HBM = pl.BlockSpec(memory_space=pltpu.HBM)
PARAMS = pltpu.CompilerParams(vmem_limit_bytes=16 * 2**20)


def log2(x):
    return jnp.log(x) * LOG2E


def join(x):
    peak = jnp.max(x, axis=0)
    return peak + log2(jnp.sum(jnp.exp2(x - peak[None]), axis=0))


def join_kernel(x_ref, out_ref):
    strips = out_ref.shape[-2]
    out_ref[...] = jnp.broadcast_to(join(x_ref[:, pl.ds(0, strips), :]), out_ref.shape)


def joined(x, *shape):
    return pl.pallas_call(
        join_kernel,
        compiler_params=PARAMS,
        out_shape=jax.ShapeDtypeStruct(shape, jnp.float32),
        in_specs=[VMEM],
        out_specs=VMEM,
    )(x)


def strip(s):
    return pl.ds(s * LANES, LANES)


def spread_rows(scale_ref, pace):
    for h in range(scale_ref.shape[0] // LANES):
        row = jnp.broadcast_to(pace[h : h + 1, :] * UNIT, (LANES, LANES))
        scale_ref[strip(h), :] = row.T


def strip_lse(s, v, scale_ref, weighted_ref):
    y = v.astype(jnp.float32) * scale_ref[...]
    top = jnp.max(y, axis=0, keepdims=True)
    e = jnp.exp2(y - top)
    weighted_ref[:, strip(s)] = y * e
    return top, top + log2(jnp.sum(e, axis=0, keepdims=True))


def first_kernel(
    values_hbm, pace_hbm, limits_hbm, reserve_hbm,
    send_ref, top_ref, weighted_ref, values_ref, wide_ref, reserve_ref,
    pace_ref, limits_ref, scale_ref, sems,
):
    rows, columns = values_ref.shape
    strips, halves = columns // LANES, rows // LANES
    width = columns // CHUNKS
    pairs = ((pace_hbm, pace_ref), (limits_hbm, limits_ref), (reserve_hbm, reserve_ref))
    small = [pltpu.make_async_copy(a, b, sems.at[CHUNKS + n]) for n, (a, b) in enumerate(pairs)]
    small[0].start()
    copies = []
    for c in range(CHUNKS):
        part = pl.ds(c * width, width)
        copies.append(pltpu.make_async_copy(values_hbm.at[:, part], values_ref.at[:, part], sems.at[c]))
        copies[c].start()
    small[1].start()
    small[2].start()
    small[0].wait()
    send_ref[pl.ds(strips, halves), :] = pace_ref[...]
    spread_rows(scale_ref, pace_ref[...])
    per = width // LANES
    for c in range(CHUNKS):
        copies[c].wait()
        for s in range(c * per, (c + 1) * per):
            v = values_ref[:, strip(s)].astype(jnp.float32)
            wide_ref[:, strip(s)] = v
            top, lse = strip_lse(s, v, scale_ref, weighted_ref)
            top_ref[pl.ds(s, 1), :] = top
            send_ref[pl.ds(s, 1), :] = lse
    small[1].wait()
    send_ref[pl.ds(strips + halves, halves), :] = limits_ref[...]
    send_ref[pl.ds(strips + 2 * halves, 4), :] = jnp.zeros((4, LANES), jnp.float32)
    small[2].wait()


def new_pace(parts, pace, limits):
    spend = jnp.sum(parts, axis=0) * BACK
    return jnp.minimum(1.0, pace * jnp.sqrt(limits / spend))


def next_kernel(
    values_ref, other_ref, parts_ref, send_ref, pair_ref,
    pace_out, limits_out, lse_ref, top_ref, weighted_ref, scale_ref,
):
    rows, columns = values_ref.shape
    strips, halves = columns // LANES, rows // LANES
    both = 2 * halves
    mine = send_ref[pl.ds(strips, both), :]
    theirs = pair_ref[0, pl.ds(strips, both), :]
    pace = jnp.concatenate([mine[:halves], theirs[:halves]], axis=0)
    limits = jnp.concatenate([mine[halves:], theirs[halves:]], axis=0)
    pace = new_pace(parts_ref[...], pace, limits)
    pace_out[...] = pace
    limits_out[...] = limits
    ends = []
    for k, source in enumerate((values_ref, other_ref)):
        block = pl.ds(k * rows, rows)
        spread_rows(scale_ref.at[block], pace[k * halves : (k + 1) * halves])
    for s in range(strips):
        for k, source in enumerate((values_ref, other_ref)):
            block = pl.ds(k * rows, rows)
            top, lse = strip_lse(s, source[:, strip(s)], scale_ref.at[block], weighted_ref.at[block])
            top_ref[k, pl.ds(s, 1), :] = top
            ends.append(lse)
        one, two = ends[-2:]
        peak = jnp.maximum(one, two)
        lse_ref[pl.ds(s, 1), :] = peak + log2(jnp.exp2(one - peak) + jnp.exp2(two - peak))


def total_lse(z_ref, reserve_ref):
    rlog = reserve_ref[...] * UNIT
    peak = jnp.maximum(jnp.max(z_ref[...], axis=0), rlog)
    total = jnp.sum(jnp.exp2(z_ref[...] - peak[None]), axis=0) + jnp.exp2(rlog - peak)
    return peak + log2(total)


def put_parts(parts_ref, first, acc):
    for h in range(acc.shape[0] // LANES):
        part = jnp.sum(acc[h * LANES : (h + 1) * LANES, :].T, axis=0, keepdims=True)
        parts_ref[:, pl.ds(first + h, 1), :] = jnp.broadcast_to(part[None], (parts_ref.shape[0], 1, LANES))


def weighted_sums(weighted_ref, block, w):
    acc = weighted_ref[block, strip(0)] * w[0:1, :]
    for s in range(1, w.shape[0]):
        acc = acc + weighted_ref[block, strip(s)] * w[s : s + 1, :]
    return acc


def spend_kernel(z_ref, reserve_ref, top_ref, weighted_ref, other_ref, pair_ref, parts_ref, scale_ref):
    rows, columns = weighted_ref.shape
    strips, halves = columns // LANES, rows // LANES
    lse = total_lse(z_ref, reserve_ref)
    spread_rows(scale_ref, pair_ref[0, pl.ds(strips, halves), :])
    put_parts(parts_ref, 0, weighted_sums(weighted_ref, pl.ds(0, rows), jnp.exp2(top_ref[...] - lse)))
    for h in range(halves):
        acc = jnp.zeros((LANES, LANES), jnp.float32)
        for s in range(strips):
            y = other_ref[strip(h), strip(s)] * scale_ref[strip(h), :]
            acc = acc + y * jnp.exp2(y - lse[s : s + 1, :])
        put_parts(parts_ref, halves + h, acc)


def last_spend_kernel(z_ref, reserve_ref, top_ref, weighted_ref, parts_ref, prices_ref):
    rows = weighted_ref.shape[0] // 2
    lse = total_lse(z_ref, reserve_ref)
    prices_ref[...] = BACK * lse
    for k in range(2):
        w = jnp.exp2(top_ref[k] - lse)
        put_parts(parts_ref, k * (rows // LANES), weighted_sums(weighted_ref, pl.ds(k * rows, rows), w))


def pack_kernel(parts_ref, pace_ref, limits_ref, prices_ref, out_ref):
    strips, both = prices_ref.shape[0], pace_ref.shape[0]
    out_ref[pl.ds(0, strips), :] = prices_ref[...]
    out_ref[pl.ds(strips, both), :] = new_pace(parts_ref[...], pace_ref[...], limits_ref[...])
    out_ref[pl.ds(strips + both, 8 - both), :] = jnp.zeros((8 - both, LANES), jnp.float32)


def pick_kernel(pair_ref, pace_ref, prices_ref):
    strips, halves = prices_ref.shape[0], pace_ref.shape[0]
    prices_ref[...] = pair_ref[1, pl.ds(0, strips), :]
    second = lax.axis_index("adv") % CORES == 1
    mine = pair_ref[1, pl.ds(strips, halves), :]
    theirs = pair_ref[1, pl.ds(strips + halves, halves), :]
    pace_ref[...] = jnp.where(second, mine, theirs)


def f32(*shape):
    return jax.ShapeDtypeStruct(shape, jnp.float32)


def on_device(groups, values, limits, start_pace, reserve):
    rows, columns = values.shape
    imp = lax.axis_size("imp")
    far = lax.axis_size("adv") // NEAR
    strips, halves = columns // LANES, rows // LANES
    both = 2 * halves
    args = (values, start_pace.reshape(halves, LANES), limits.reshape(halves, LANES), reserve.reshape(strips, LANES))
    args = [pltpu.with_memory_space_constraint(a, pltpu.HBM) for a in args]

    def along_z(own):
        own = joined(lax.all_gather(own, "adv", axis_index_groups=groups["chips"]), far, strips, LANES)
        return lax.all_to_all(own, ("adv", "imp"), 0, 0, axis_index_groups=groups["z"], tiled=True)

    send, top, weighted, values, wide, reserve = pl.pallas_call(
        first_kernel,
        compiler_params=PARAMS,
        out_shape=(
            f32(strips + 2 * halves + 4, LANES),
            f32(strips, LANES),
            f32(rows, columns),
            jax.ShapeDtypeStruct((rows, columns), values.dtype),
            f32(rows, columns),
            f32(strips, LANES),
        ),
        in_specs=[HBM] * 4,
        out_specs=(VMEM,) * 6,
        scratch_shapes=[
            pltpu.VMEM((halves, LANES), jnp.float32),
            pltpu.VMEM((halves, LANES), jnp.float32),
            pltpu.VMEM((rows, LANES), jnp.float32),
            pltpu.SemaphoreType.DMA((CHUNKS + 3,)),
        ],
    )(*args)
    pair = lax.all_gather(send, "adv", axis_index_groups=groups["cores"])
    wide, pair = lax.optimization_barrier((wide, pair))
    other = lax.ppermute(wide, "adv", groups["ship"])
    parts = pl.pallas_call(
        spend_kernel,
        compiler_params=PARAMS,
        out_shape=f32(imp, both, LANES),
        in_specs=[VMEM] * 6,
        out_specs=VMEM,
        scratch_shapes=[pltpu.VMEM((rows, LANES), jnp.float32)],
    )(along_z(joined(pair, strips, LANES)), reserve, top, weighted, other, pair)
    parts = lax.all_to_all(parts, "imp", 0, 0, axis_index_groups=groups["imp"], tiled=True)
    pace, limits, own, top, weighted = pl.pallas_call(
        next_kernel,
        compiler_params=PARAMS,
        out_shape=(
            f32(both, LANES),
            f32(both, LANES),
            f32(strips, LANES),
            f32(2, strips, LANES),
            f32(2 * rows, columns),
        ),
        in_specs=[VMEM] * 5,
        out_specs=(VMEM,) * 5,
        scratch_shapes=[pltpu.VMEM((2 * rows, LANES), jnp.float32)],
    )(values, other, parts, send, pair)
    parts, prices = pl.pallas_call(
        last_spend_kernel,
        compiler_params=PARAMS,
        out_shape=(f32(imp, both, LANES), f32(strips, LANES)),
        in_specs=[VMEM] * 4,
        out_specs=(VMEM, VMEM),
    )(along_z(own), reserve, top, weighted)
    parts = lax.all_to_all(parts, "imp", 0, 0, axis_index_groups=groups["imp"], tiled=True)
    done = pl.pallas_call(
        pack_kernel,
        compiler_params=PARAMS,
        out_shape=f32(strips + 8, LANES),
        in_specs=[VMEM] * 4,
        out_specs=VMEM,
    )(parts, pace, limits, prices)
    pace, prices = pl.pallas_call(
        pick_kernel,
        compiler_params=PARAMS,
        out_shape=(f32(halves, LANES), f32(strips, LANES)),
        in_specs=[VMEM],
        out_specs=(VMEM, VMEM),
    )(lax.all_gather(done, "adv", axis_index_groups=groups["cores"]))
    return (pace.reshape(rows), prices.reshape(columns))


def solution(mesh):
    placed = (P("adv", "imp"), P("adv"), P("adv"), P("imp"))
    adv, imp = mesh.shape["adv"], mesh.shape["imp"]
    far, chips = adv // NEAR, NEAR // CORES

    def at(z, chip, core):
        return z * NEAR + chip * CORES + core

    order = [(z + FIRST_Z) % far for z in range(far)]
    along_z = [[at(z, c, 1) * imp + i for z in order] for c in range(chips) for i in range(imp)]
    plane = [at(z, c, 0) * imp + i for z in range(far) for c in range(chips) for i in range(imp)]
    groups = dict(
        cores=[[at(z, c, k) for k in range(CORES)] for z in range(far) for c in range(chips)],
        chips=[[at(z, c, k) for c in range(chips)] for z in range(far) for k in range(CORES)],
        ship=[(at(z, c, 0), at(z, c, 1)) for z in range(far) for c in range(chips)],
        imp=[[(i + FIRST_IMP) % imp for i in range(imp)]],
        z=along_z + [plane[n : n + far] for n in range(0, len(plane), far)],
    )

    def step(*args):
        return on_device(groups, *args)

    return jax.shard_map(
        step, mesh=mesh, in_specs=placed, out_specs=(P("adv"), P("imp")), check_vma=False
    )
```

```python
import math

import jax
import jax.numpy as jnp
from jax import lax
from jax.experimental import pallas as pl
from jax.experimental.pallas import tpu as pltpu
from jax.sharding import PartitionSpec as P

EPS = 0.015
CORES = 2
NEAR = 4
LANES = 128
CHUNKS = 4
ORDER_Z = (9, 0, 1, 2, 3, 15, 14, 4, 5, 6, 7, 13, 12, 11, 10, 8)
ORDER_IMP = (5, 0, 2, 6, 1, 3, 7, 4)
UNIT = math.log2(math.e) / EPS
BACK = EPS / math.log2(math.e)
LOG2E = math.log2(math.e)

VMEM = pl.BlockSpec(memory_space=pltpu.VMEM)
HBM = pl.BlockSpec(memory_space=pltpu.HBM)
PARAMS = pltpu.CompilerParams(vmem_limit_bytes=16 * 2**20)


def log2(x):
    return jnp.log(x) * LOG2E


def join(x):
    peak = jnp.max(x, axis=0)
    return peak + log2(jnp.sum(jnp.exp2(x - peak[None]), axis=0))


def join_kernel(x_ref, out_ref):
    strips = out_ref.shape[-2]
    out_ref[...] = jnp.broadcast_to(join(x_ref[:, pl.ds(0, strips), :]), out_ref.shape)


def joined(x, *shape):
    return pl.pallas_call(
        join_kernel,
        compiler_params=PARAMS,
        out_shape=jax.ShapeDtypeStruct(shape, jnp.float32),
        in_specs=[VMEM],
        out_specs=VMEM,
    )(x)


def strip(s):
    return pl.ds(s * LANES, LANES)


def spread_rows(scale_ref, pace):
    for h in range(scale_ref.shape[0] // LANES):
        row = jnp.broadcast_to(pace[h : h + 1, :] * UNIT, (LANES, LANES))
        scale_ref[strip(h), :] = row.T


def strip_lse(s, v, scale_ref, weighted_ref):
    y = v.astype(jnp.float32) * scale_ref[...]
    top = jnp.max(y, axis=0, keepdims=True)
    e = jnp.exp2(y - top)
    weighted_ref[:, strip(s)] = y * e
    return top, top + log2(jnp.sum(e, axis=0, keepdims=True))


def first_kernel(
    values_hbm, pace_hbm, limits_hbm, reserve_hbm,
    send_ref, top_ref, weighted_ref, values_ref, wide_ref, reserve_ref,
    pace_ref, limits_ref, scale_ref, sems,
):
    rows, columns = values_ref.shape
    strips, halves = columns // LANES, rows // LANES
    width = columns // CHUNKS
    pairs = ((pace_hbm, pace_ref), (limits_hbm, limits_ref), (reserve_hbm, reserve_ref))
    small = [pltpu.make_async_copy(a, b, sems.at[CHUNKS + n]) for n, (a, b) in enumerate(pairs)]
    small[0].start()
    copies = []
    for c in range(CHUNKS):
        part = pl.ds(c * width, width)
        copies.append(pltpu.make_async_copy(values_hbm.at[:, part], values_ref.at[:, part], sems.at[c]))
        copies[c].start()
    small[1].start()
    small[2].start()
    small[0].wait()
    send_ref[pl.ds(strips, halves), :] = pace_ref[...]
    spread_rows(scale_ref, pace_ref[...])
    per = width // LANES
    for c in range(CHUNKS):
        copies[c].wait()
        for s in range(c * per, (c + 1) * per):
            v = values_ref[:, strip(s)].astype(jnp.float32)
            wide_ref[:, strip(s)] = v
            top, lse = strip_lse(s, v, scale_ref, weighted_ref)
            top_ref[pl.ds(s, 1), :] = top
            send_ref[pl.ds(s, 1), :] = lse
    small[1].wait()
    send_ref[pl.ds(strips + halves, halves), :] = limits_ref[...]
    send_ref[pl.ds(strips + 2 * halves, 4), :] = jnp.zeros((4, LANES), jnp.float32)
    small[2].wait()


def new_pace(parts, pace, limits):
    spend = jnp.sum(parts, axis=0) * BACK
    return jnp.minimum(1.0, pace * jnp.sqrt(limits / spend))


def next_kernel(
    values_ref, other_ref, parts_ref, send_ref, pair_ref,
    pace_out, limits_out, lse_ref, top_ref, weighted_ref, scale_ref,
):
    rows, columns = values_ref.shape
    strips, halves = columns // LANES, rows // LANES
    both = 2 * halves
    mine = send_ref[pl.ds(strips, both), :]
    theirs = pair_ref[0, pl.ds(strips, both), :]
    pace = jnp.concatenate([mine[:halves], theirs[:halves]], axis=0)
    limits = jnp.concatenate([mine[halves:], theirs[halves:]], axis=0)
    pace = new_pace(parts_ref[...], pace, limits)
    pace_out[...] = pace
    limits_out[...] = limits
    ends = []
    for k, source in enumerate((values_ref, other_ref)):
        block = pl.ds(k * rows, rows)
        spread_rows(scale_ref.at[block], pace[k * halves : (k + 1) * halves])
    for s in range(strips):
        for k, source in enumerate((values_ref, other_ref)):
            block = pl.ds(k * rows, rows)
            top, lse = strip_lse(s, source[:, strip(s)], scale_ref.at[block], weighted_ref.at[block])
            top_ref[k, pl.ds(s, 1), :] = top
            ends.append(lse)
        one, two = ends[-2:]
        peak = jnp.maximum(one, two)
        lse_ref[pl.ds(s, 1), :] = peak + log2(jnp.exp2(one - peak) + jnp.exp2(two - peak))


def total_lse(z_ref, reserve_ref):
    rlog = reserve_ref[...] * UNIT
    peak = jnp.maximum(jnp.max(z_ref[...], axis=0), rlog)
    total = jnp.sum(jnp.exp2(z_ref[...] - peak[None]), axis=0) + jnp.exp2(rlog - peak)
    return peak + log2(total)


def put_parts(parts_ref, first, acc):
    for h in range(acc.shape[0] // LANES):
        part = jnp.sum(acc[h * LANES : (h + 1) * LANES, :].T, axis=0, keepdims=True)
        parts_ref[:, pl.ds(first + h, 1), :] = jnp.broadcast_to(part[None], (parts_ref.shape[0], 1, LANES))


def weighted_sums(weighted_ref, block, w):
    acc = weighted_ref[block, strip(0)] * w[0:1, :]
    for s in range(1, w.shape[0]):
        acc = acc + weighted_ref[block, strip(s)] * w[s : s + 1, :]
    return acc


def spend_kernel(z_ref, reserve_ref, top_ref, weighted_ref, other_ref, pair_ref, parts_ref, scale_ref):
    rows, columns = weighted_ref.shape
    strips, halves = columns // LANES, rows // LANES
    lse = total_lse(z_ref, reserve_ref)
    spread_rows(scale_ref, pair_ref[0, pl.ds(strips, halves), :])
    put_parts(parts_ref, 0, weighted_sums(weighted_ref, pl.ds(0, rows), jnp.exp2(top_ref[...] - lse)))
    for h in range(halves):
        acc = jnp.zeros((LANES, LANES), jnp.float32)
        for s in range(strips):
            y = other_ref[strip(h), strip(s)] * scale_ref[strip(h), :]
            acc = acc + y * jnp.exp2(y - lse[s : s + 1, :])
        put_parts(parts_ref, halves + h, acc)


def last_spend_kernel(z_ref, reserve_ref, top_ref, weighted_ref, parts_ref, prices_ref):
    rows = weighted_ref.shape[0] // 2
    lse = total_lse(z_ref, reserve_ref)
    prices_ref[...] = BACK * lse
    for k in range(2):
        w = jnp.exp2(top_ref[k] - lse)
        put_parts(parts_ref, k * (rows // LANES), weighted_sums(weighted_ref, pl.ds(k * rows, rows), w))


def pack_kernel(parts_ref, pace_ref, limits_ref, prices_ref, out_ref):
    strips, both = prices_ref.shape[0], pace_ref.shape[0]
    out_ref[pl.ds(0, strips), :] = prices_ref[...]
    out_ref[pl.ds(strips, both), :] = new_pace(parts_ref[...], pace_ref[...], limits_ref[...])
    out_ref[pl.ds(strips + both, 8 - both), :] = jnp.zeros((8 - both, LANES), jnp.float32)


def pick_kernel(pair_ref, pace_ref, prices_ref):
    strips, halves = prices_ref.shape[0], pace_ref.shape[0]
    prices_ref[...] = pair_ref[1, pl.ds(0, strips), :]
    second = lax.axis_index("adv") % CORES == 1
    mine = pair_ref[1, pl.ds(strips, halves), :]
    theirs = pair_ref[1, pl.ds(strips + halves, halves), :]
    pace_ref[...] = jnp.where(second, mine, theirs)


def f32(*shape):
    return jax.ShapeDtypeStruct(shape, jnp.float32)


def on_device(groups, values, limits, start_pace, reserve):
    rows, columns = values.shape
    imp = lax.axis_size("imp")
    far = lax.axis_size("adv") // NEAR
    strips, halves = columns // LANES, rows // LANES
    both = 2 * halves
    args = (values, start_pace.reshape(halves, LANES), limits.reshape(halves, LANES), reserve.reshape(strips, LANES))
    args = [pltpu.with_memory_space_constraint(a, pltpu.HBM) for a in args]

    def along_z(own):
        own = joined(lax.all_gather(own, "adv", axis_index_groups=groups["chips"]), far, strips, LANES)
        return lax.all_to_all(own, ("adv", "imp"), 0, 0, axis_index_groups=groups["z"], tiled=True)

    send, top, weighted, values, wide, reserve = pl.pallas_call(
        first_kernel,
        compiler_params=PARAMS,
        out_shape=(
            f32(strips + 2 * halves + 4, LANES),
            f32(strips, LANES),
            f32(rows, columns),
            jax.ShapeDtypeStruct((rows, columns), values.dtype),
            f32(rows, columns),
            f32(strips, LANES),
        ),
        in_specs=[HBM] * 4,
        out_specs=(VMEM,) * 6,
        scratch_shapes=[
            pltpu.VMEM((halves, LANES), jnp.float32),
            pltpu.VMEM((halves, LANES), jnp.float32),
            pltpu.VMEM((rows, LANES), jnp.float32),
            pltpu.SemaphoreType.DMA((CHUNKS + 3,)),
        ],
    )(*args)
    pair = lax.all_gather(send, "adv", axis_index_groups=groups["cores"])
    wide, pair = lax.optimization_barrier((wide, pair))
    other = lax.ppermute(wide, "adv", groups["ship"])
    parts = pl.pallas_call(
        spend_kernel,
        compiler_params=PARAMS,
        out_shape=f32(imp, both, LANES),
        in_specs=[VMEM] * 6,
        out_specs=VMEM,
        scratch_shapes=[pltpu.VMEM((rows, LANES), jnp.float32)],
    )(along_z(joined(pair, strips, LANES)), reserve, top, weighted, other, pair)
    parts = lax.all_to_all(parts, "imp", 0, 0, axis_index_groups=groups["imp"], tiled=True)
    pace, limits, own, top, weighted = pl.pallas_call(
        next_kernel,
        compiler_params=PARAMS,
        out_shape=(
            f32(both, LANES),
            f32(both, LANES),
            f32(strips, LANES),
            f32(2, strips, LANES),
            f32(2 * rows, columns),
        ),
        in_specs=[VMEM] * 5,
        out_specs=(VMEM,) * 5,
        scratch_shapes=[pltpu.VMEM((2 * rows, LANES), jnp.float32)],
    )(values, other, parts, send, pair)
    parts, prices = pl.pallas_call(
        last_spend_kernel,
        compiler_params=PARAMS,
        out_shape=(f32(imp, both, LANES), f32(strips, LANES)),
        in_specs=[VMEM] * 4,
        out_specs=(VMEM, VMEM),
    )(along_z(own), reserve, top, weighted)
    parts = lax.all_to_all(parts, "imp", 0, 0, axis_index_groups=groups["imp"], tiled=True)
    done = pl.pallas_call(
        pack_kernel,
        compiler_params=PARAMS,
        out_shape=f32(strips + 8, LANES),
        in_specs=[VMEM] * 4,
        out_specs=VMEM,
    )(parts, pace, limits, prices)
    pace, prices = pl.pallas_call(
        pick_kernel,
        compiler_params=PARAMS,
        out_shape=(f32(halves, LANES), f32(strips, LANES)),
        in_specs=[VMEM],
        out_specs=(VMEM, VMEM),
    )(lax.all_gather(done, "adv", axis_index_groups=groups["cores"]))
    return (pace.reshape(rows), prices.reshape(columns))


def solution(mesh):
    placed = (P("adv", "imp"), P("adv"), P("adv"), P("imp"))
    adv, imp = mesh.shape["adv"], mesh.shape["imp"]
    far, chips = adv // NEAR, NEAR // CORES

    def at(z, chip, core):
        return z * NEAR + chip * CORES + core

    order = ORDER_Z if far == len(ORDER_Z) else range(far)
    over_imp = ORDER_IMP if imp == len(ORDER_IMP) else range(imp)
    along_z = [[at(z, c, 1) * imp + i for z in order] for c in range(chips) for i in range(imp)]
    plane = [at(z, c, 0) * imp + i for z in range(far) for c in range(chips) for i in range(imp)]
    groups = dict(
        cores=[[at(z, c, k) for k in range(CORES)] for z in range(far) for c in range(chips)],
        chips=[[at(z, c, k) for c in range(chips)] for z in range(far) for k in range(CORES)],
        ship=[(at(z, c, 0), at(z, c, 1)) for z in range(far) for c in range(chips)],
        imp=[list(over_imp)],
        z=along_z + [plane[n : n + far] for n in range(0, len(plane), far)],
    )

    def step(*args):
        return on_device(groups, *args)

    return jax.shard_map(
        step, mesh=mesh, in_specs=placed, out_specs=(P("adv"), P("imp")), check_vma=False
    )
```

```python
import math

import jax
import jax.numpy as jnp
from jax import lax
from jax.experimental import pallas as pl
from jax.experimental.pallas import tpu as pltpu
from jax.sharding import PartitionSpec as P

EPS = 0.015
CORES = 2
NEAR = 4
LANES = 128
CHUNKS = 4
ORDER_Z = (9, 0, 1, 2, 3, 15, 14, 4, 5, 6, 7, 13, 12, 11, 10, 8)
ORDER_IMP = (5, 0, 2, 6, 1, 3, 7, 4)
UNIT = math.log2(math.e) / EPS
BACK = EPS / math.log2(math.e)
LOG2E = math.log2(math.e)

VMEM = pl.BlockSpec(memory_space=pltpu.VMEM)
HBM = pl.BlockSpec(memory_space=pltpu.HBM)
PARAMS = pltpu.CompilerParams(vmem_limit_bytes=16 * 2**20)


def log2(x):
    return jnp.log(x) * LOG2E


def join(x):
    peak = jnp.max(x, axis=0)
    return peak + log2(jnp.sum(jnp.exp2(x - peak[None]), axis=0))


def join_kernel(x_ref, out_ref):
    strips = out_ref.shape[-2]
    out_ref[...] = jnp.broadcast_to(join(x_ref[:, pl.ds(0, strips), :]), out_ref.shape)


def joined(x, *shape):
    return pl.pallas_call(
        join_kernel,
        compiler_params=PARAMS,
        out_shape=jax.ShapeDtypeStruct(shape, jnp.float32),
        in_specs=[VMEM],
        out_specs=VMEM,
    )(x)


def strip(s):
    return pl.ds(s * LANES, LANES)


def spread_rows(scale_ref, pace):
    for h in range(scale_ref.shape[0] // LANES):
        row = jnp.broadcast_to(pace[h : h + 1, :] * UNIT, (LANES, LANES))
        scale_ref[strip(h), :] = row.T


def strip_lse(s, v, scale_ref, weighted_ref):
    y = v.astype(jnp.float32) * scale_ref[...]
    top = jnp.max(y, axis=0, keepdims=True)
    e = jnp.exp2(y - top)
    weighted_ref[:, strip(s)] = y * e
    return top, top + log2(jnp.sum(e, axis=0, keepdims=True))


def first_kernel(
    values_hbm, pace_hbm, limits_hbm, reserve_hbm,
    send_ref, top_ref, weighted_ref, values_ref, wide_ref, reserve_ref,
    pace_ref, limits_ref, scale_ref, sems,
):
    rows, columns = values_ref.shape
    strips, halves = columns // LANES, rows // LANES
    width = columns // CHUNKS
    pairs = ((pace_hbm, pace_ref), (limits_hbm, limits_ref), (reserve_hbm, reserve_ref))
    small = [pltpu.make_async_copy(a, b, sems.at[CHUNKS + n]) for n, (a, b) in enumerate(pairs)]
    small[0].start()
    copies = []
    for c in range(CHUNKS):
        part = pl.ds(c * width, width)
        copies.append(pltpu.make_async_copy(values_hbm.at[:, part], values_ref.at[:, part], sems.at[c]))
        copies[c].start()
    small[1].start()
    small[2].start()
    small[0].wait()
    send_ref[pl.ds(strips, halves), :] = pace_ref[...]
    spread_rows(scale_ref, pace_ref[...])
    per = width // LANES
    for c in range(CHUNKS):
        copies[c].wait()
        for s in range(c * per, (c + 1) * per):
            v = values_ref[:, strip(s)].astype(jnp.float32)
            wide_ref[:, strip(s)] = v
            top, lse = strip_lse(s, v, scale_ref, weighted_ref)
            top_ref[pl.ds(s, 1), :] = top
            send_ref[pl.ds(s, 1), :] = lse
    small[1].wait()
    send_ref[pl.ds(strips + halves, halves), :] = limits_ref[...]
    send_ref[pl.ds(strips + 2 * halves, 4), :] = jnp.zeros((4, LANES), jnp.float32)
    small[2].wait()


def new_pace(parts, pace, limits):
    spend = jnp.sum(parts, axis=0) * BACK
    return jnp.minimum(1.0, pace * jnp.sqrt(limits / spend))


def next_kernel(
    values_ref, other_ref, parts_ref, send_ref, pair_ref,
    pace_out, limits_out, lse_ref, top_ref, weighted_ref, scale_ref,
):
    rows, columns = values_ref.shape
    strips, halves = columns // LANES, rows // LANES
    both = 2 * halves
    mine = send_ref[pl.ds(strips, both), :]
    theirs = pair_ref[1, pl.ds(strips, both), :]
    pace = jnp.concatenate([mine[:halves], theirs[:halves]], axis=0)
    limits = jnp.concatenate([mine[halves:], theirs[halves:]], axis=0)
    pace = new_pace(parts_ref[...], pace, limits)
    pace_out[...] = pace
    limits_out[...] = limits
    ends = []
    for k, source in enumerate((values_ref, other_ref)):
        block = pl.ds(k * rows, rows)
        spread_rows(scale_ref.at[block], pace[k * halves : (k + 1) * halves])
    for s in range(strips):
        for k, source in enumerate((values_ref, other_ref)):
            block = pl.ds(k * rows, rows)
            top, lse = strip_lse(s, source[:, strip(s)], scale_ref.at[block], weighted_ref.at[block])
            top_ref[k, pl.ds(s, 1), :] = top
            ends.append(lse)
        one, two = ends[-2:]
        peak = jnp.maximum(one, two)
        lse_ref[pl.ds(s, 1), :] = peak + log2(jnp.exp2(one - peak) + jnp.exp2(two - peak))


def total_lse(z_ref, reserve_ref):
    rlog = reserve_ref[...] * UNIT
    peak = jnp.maximum(jnp.max(z_ref[...], axis=0), rlog)
    total = jnp.sum(jnp.exp2(z_ref[...] - peak[None]), axis=0) + jnp.exp2(rlog - peak)
    return peak + log2(total)


def put_parts(parts_ref, first, acc):
    for h in range(acc.shape[0] // LANES):
        part = jnp.sum(acc[h * LANES : (h + 1) * LANES, :].T, axis=0, keepdims=True)
        parts_ref[:, pl.ds(first + h, 1), :] = jnp.broadcast_to(part[None], (parts_ref.shape[0], 1, LANES))


def weighted_sums(weighted_ref, block, w):
    acc = weighted_ref[block, strip(0)] * w[0:1, :]
    for s in range(1, w.shape[0]):
        acc = acc + weighted_ref[block, strip(s)] * w[s : s + 1, :]
    return acc


def spend_kernel(z_ref, reserve_ref, top_ref, weighted_ref, other_ref, pair_ref, parts_ref, scale_ref):
    rows, columns = weighted_ref.shape
    strips, halves = columns // LANES, rows // LANES
    lse = total_lse(z_ref, reserve_ref)
    spread_rows(scale_ref, pair_ref[1, pl.ds(strips, halves), :])
    put_parts(parts_ref, 0, weighted_sums(weighted_ref, pl.ds(0, rows), jnp.exp2(top_ref[...] - lse)))
    for h in range(halves):
        acc = jnp.zeros((LANES, LANES), jnp.float32)
        for s in range(strips):
            y = other_ref[strip(h), strip(s)] * scale_ref[strip(h), :]
            acc = acc + y * jnp.exp2(y - lse[s : s + 1, :])
        put_parts(parts_ref, halves + h, acc)


def last_spend_kernel(z_ref, reserve_ref, top_ref, weighted_ref, parts_ref, prices_ref):
    rows = weighted_ref.shape[0] // 2
    lse = total_lse(z_ref, reserve_ref)
    prices_ref[...] = BACK * lse
    for k in range(2):
        w = jnp.exp2(top_ref[k] - lse)
        put_parts(parts_ref, k * (rows // LANES), weighted_sums(weighted_ref, pl.ds(k * rows, rows), w))


def pack_kernel(parts_ref, pace_ref, limits_ref, prices_ref, out_ref):
    strips, both = prices_ref.shape[0], pace_ref.shape[0]
    out_ref[pl.ds(0, strips), :] = prices_ref[...]
    out_ref[pl.ds(strips, both), :] = new_pace(parts_ref[...], pace_ref[...], limits_ref[...])
    out_ref[pl.ds(strips + both, 8 - both), :] = jnp.zeros((8 - both, LANES), jnp.float32)


def pick_kernel(pair_ref, pace_ref, prices_ref):
    strips, halves = prices_ref.shape[0], pace_ref.shape[0]
    prices_ref[...] = pair_ref[0, pl.ds(0, strips), :]
    second = lax.axis_index("adv") % CORES == 1
    mine = pair_ref[0, pl.ds(strips, halves), :]
    theirs = pair_ref[0, pl.ds(strips + halves, halves), :]
    pace_ref[...] = jnp.where(second, mine, theirs)


def f32(*shape):
    return jax.ShapeDtypeStruct(shape, jnp.float32)


def on_device(groups, values, limits, start_pace, reserve):
    rows, columns = values.shape
    imp = lax.axis_size("imp")
    far = lax.axis_size("adv") // NEAR
    strips, halves = columns // LANES, rows // LANES
    both = 2 * halves
    args = (values, start_pace.reshape(halves, LANES), limits.reshape(halves, LANES), reserve.reshape(strips, LANES))
    args = [pltpu.with_memory_space_constraint(a, pltpu.HBM) for a in args]

    def along_z(own):
        own = joined(lax.all_gather(own, "adv", axis_index_groups=groups["chips"]), far, strips, LANES)
        return lax.all_to_all(own, ("adv", "imp"), 0, 0, axis_index_groups=groups["z"], tiled=True)

    send, top, weighted, values, wide, reserve = pl.pallas_call(
        first_kernel,
        compiler_params=PARAMS,
        out_shape=(
            f32(strips + 2 * halves + 4, LANES),
            f32(strips, LANES),
            f32(rows, columns),
            jax.ShapeDtypeStruct((rows, columns), values.dtype),
            f32(rows, columns),
            f32(strips, LANES),
        ),
        in_specs=[HBM] * 4,
        out_specs=(VMEM,) * 6,
        scratch_shapes=[
            pltpu.VMEM((halves, LANES), jnp.float32),
            pltpu.VMEM((halves, LANES), jnp.float32),
            pltpu.VMEM((rows, LANES), jnp.float32),
            pltpu.SemaphoreType.DMA((CHUNKS + 3,)),
        ],
    )(*args)
    pair = lax.all_gather(send, "adv", axis_index_groups=groups["cores"])
    wide, pair = lax.optimization_barrier((wide, pair))
    other = lax.ppermute(wide, "adv", groups["ship"])
    parts = pl.pallas_call(
        spend_kernel,
        compiler_params=PARAMS,
        out_shape=f32(imp, both, LANES),
        in_specs=[VMEM] * 6,
        out_specs=VMEM,
        scratch_shapes=[pltpu.VMEM((rows, LANES), jnp.float32)],
    )(along_z(joined(pair, strips, LANES)), reserve, top, weighted, other, pair)
    parts = lax.all_to_all(parts, "imp", 0, 0, axis_index_groups=groups["imp"], tiled=True)
    pace, limits, own, top, weighted = pl.pallas_call(
        next_kernel,
        compiler_params=PARAMS,
        out_shape=(
            f32(both, LANES),
            f32(both, LANES),
            f32(strips, LANES),
            f32(2, strips, LANES),
            f32(2 * rows, columns),
        ),
        in_specs=[VMEM] * 5,
        out_specs=(VMEM,) * 5,
        scratch_shapes=[pltpu.VMEM((2 * rows, LANES), jnp.float32)],
    )(values, other, parts, send, pair)
    parts, prices = pl.pallas_call(
        last_spend_kernel,
        compiler_params=PARAMS,
        out_shape=(f32(imp, both, LANES), f32(strips, LANES)),
        in_specs=[VMEM] * 4,
        out_specs=(VMEM, VMEM),
    )(along_z(own), reserve, top, weighted)
    parts = lax.all_to_all(parts, "imp", 0, 0, axis_index_groups=groups["imp"], tiled=True)
    done = pl.pallas_call(
        pack_kernel,
        compiler_params=PARAMS,
        out_shape=f32(strips + 8, LANES),
        in_specs=[VMEM] * 4,
        out_specs=VMEM,
    )(parts, pace, limits, prices)
    pace, prices = pl.pallas_call(
        pick_kernel,
        compiler_params=PARAMS,
        out_shape=(f32(halves, LANES), f32(strips, LANES)),
        in_specs=[VMEM],
        out_specs=(VMEM, VMEM),
    )(lax.all_gather(done, "adv", axis_index_groups=groups["cores"]))
    return (pace.reshape(rows), prices.reshape(columns))


def solution(mesh):
    placed = (P("adv", "imp"), P("adv"), P("adv"), P("imp"))
    adv, imp = mesh.shape["adv"], mesh.shape["imp"]
    far, chips = adv // NEAR, NEAR // CORES

    def at(z, chip, core):
        return z * NEAR + chip * CORES + core

    order = ORDER_Z if far == len(ORDER_Z) else range(far)
    over_imp = ORDER_IMP if imp == len(ORDER_IMP) else range(imp)
    along_z = [[at(z, c, 1) * imp + i for z in order] for c in range(chips) for i in range(imp)]
    plane = [at(z, c, 0) * imp + i for z in range(far) for c in range(chips) for i in range(imp)]
    groups = dict(
        cores=[[at(z, c, k) for k in reversed(range(CORES))] for z in range(far) for c in range(chips)],
        chips=[[at(z, c, k) for c in range(chips)] for z in range(far) for k in range(CORES)],
        ship=[(at(z, c, 0), at(z, c, 1)) for z in range(far) for c in range(chips)],
        imp=[list(over_imp)],
        z=along_z + [plane[n : n + far] for n in range(0, len(plane), far)],
    )

    def step(*args):
        return on_device(groups, *args)

    return jax.shard_map(
        step, mesh=mesh, in_specs=placed, out_specs=(P("adv"), P("imp")), check_vma=False
    )
```

```python
import math

import jax
import jax.numpy as jnp
from jax import lax
from jax.experimental import pallas as pl
from jax.experimental.pallas import tpu as pltpu
from jax.sharding import PartitionSpec as P

EPS = 0.015
CORES = 2
NEAR = 4
LANES = 128
CHUNKS = 4
ORDER_Z = (9, 0, 1, 2, 3, 15, 14, 4, 5, 6, 7, 13, 12, 11, 10, 8)
ORDER_IMP = (5, 0, 2, 6, 1, 3, 7, 4)
UNIT = math.log2(math.e) / EPS
BACK = EPS / math.log2(math.e)
LOG2E = math.log2(math.e)

VMEM = pl.BlockSpec(memory_space=pltpu.VMEM)
HBM = pl.BlockSpec(memory_space=pltpu.HBM)
PARAMS = pltpu.CompilerParams(vmem_limit_bytes=16 * 2**20)


def log2(x):
    return jnp.log(x) * LOG2E


def join(x):
    peak = jnp.max(x, axis=0)
    return peak + log2(jnp.sum(jnp.exp2(x - peak[None]), axis=0))


def join_kernel(x_ref, out_ref):
    strips = out_ref.shape[-2]
    out_ref[...] = jnp.broadcast_to(join(x_ref[:, pl.ds(0, strips), :]), out_ref.shape)


def joined(x, *shape):
    return pl.pallas_call(
        join_kernel,
        compiler_params=PARAMS,
        out_shape=jax.ShapeDtypeStruct(shape, jnp.float32),
        in_specs=[VMEM],
        out_specs=VMEM,
    )(x)


def strip(s):
    return pl.ds(s * LANES, LANES)


def spread_rows(scale_ref, pace):
    for h in range(scale_ref.shape[0] // LANES):
        row = jnp.broadcast_to(pace[h : h + 1, :] * UNIT, (LANES, LANES))
        scale_ref[strip(h), :] = row.T


def strip_lse(s, v, scale_ref, weighted_ref):
    y = v.astype(jnp.float32) * scale_ref[...]
    top = jnp.max(y, axis=0, keepdims=True)
    e = jnp.exp2(y - top)
    weighted_ref[:, strip(s)] = y * e
    return top, top + log2(jnp.sum(e, axis=0, keepdims=True))


def first_kernel(
    values_hbm, pace_hbm, limits_hbm, reserve_hbm,
    send_ref, top_ref, weighted_ref, values_ref, wide_ref, reserve_ref,
    pace_ref, limits_ref, scale_ref, sems,
):
    rows, columns = values_ref.shape
    strips, halves = columns // LANES, rows // LANES
    width = columns // CHUNKS
    pairs = ((pace_hbm, pace_ref), (limits_hbm, limits_ref), (reserve_hbm, reserve_ref))
    small = [pltpu.make_async_copy(a, b, sems.at[CHUNKS + n]) for n, (a, b) in enumerate(pairs)]
    small[0].start()
    copies = []
    for c in range(CHUNKS):
        part = pl.ds(c * width, width)
        copies.append(pltpu.make_async_copy(values_hbm.at[:, part], values_ref.at[:, part], sems.at[c]))
        copies[c].start()
    small[1].start()
    small[2].start()
    small[0].wait()
    send_ref[pl.ds(strips, halves), :] = pace_ref[...]
    spread_rows(scale_ref, pace_ref[...])
    per = width // LANES
    for c in range(CHUNKS):
        copies[c].wait()
        for s in range(c * per, (c + 1) * per):
            v = values_ref[:, strip(s)].astype(jnp.float32)
            wide_ref[:, strip(s)] = v
            top, lse = strip_lse(s, v, scale_ref, weighted_ref)
            top_ref[pl.ds(s, 1), :] = top
            send_ref[pl.ds(s, 1), :] = lse
    small[1].wait()
    send_ref[pl.ds(strips + halves, halves), :] = limits_ref[...]
    send_ref[pl.ds(strips + 2 * halves, 4), :] = jnp.zeros((4, LANES), jnp.float32)
    small[2].wait()


def new_pace(parts, pace, limits):
    spend = jnp.sum(parts, axis=0) * BACK
    return jnp.minimum(1.0, pace * jnp.sqrt(limits / spend))


def next_kernel(
    values_ref, other_ref, parts_ref, send_ref, pair_ref,
    pace_out, limits_out, lse_ref, top_ref, weighted_ref, scale_ref,
):
    rows, columns = values_ref.shape
    strips, halves = columns // LANES, rows // LANES
    both = 2 * halves
    mine = send_ref[pl.ds(strips, both), :]
    theirs = pair_ref[0, pl.ds(strips, both), :]
    pace = jnp.concatenate([mine[:halves], theirs[:halves]], axis=0)
    limits = jnp.concatenate([mine[halves:], theirs[halves:]], axis=0)
    pace = new_pace(parts_ref[...], pace, limits)
    pace_out[...] = pace
    limits_out[...] = limits
    ends = []
    for k, source in enumerate((values_ref, other_ref)):
        block = pl.ds(k * rows, rows)
        spread_rows(scale_ref.at[block], pace[k * halves : (k + 1) * halves])
    for s in range(strips):
        for k, source in enumerate((values_ref, other_ref)):
            block = pl.ds(k * rows, rows)
            top, lse = strip_lse(s, source[:, strip(s)], scale_ref.at[block], weighted_ref.at[block])
            top_ref[k, pl.ds(s, 1), :] = top
            ends.append(lse)
        one, two = ends[-2:]
        peak = jnp.maximum(one, two)
        lse_ref[pl.ds(s, 1), :] = peak + log2(jnp.exp2(one - peak) + jnp.exp2(two - peak))


def total_lse(z_ref, reserve_ref):
    rlog = reserve_ref[...] * UNIT
    peak = jnp.maximum(jnp.max(z_ref[...], axis=0), rlog)
    total = jnp.sum(jnp.exp2(z_ref[...] - peak[None]), axis=0) + jnp.exp2(rlog - peak)
    return peak + log2(total)


def put_parts(parts_ref, first, acc):
    for h in range(acc.shape[0] // LANES):
        part = jnp.sum(acc[h * LANES : (h + 1) * LANES, :].T, axis=0, keepdims=True)
        parts_ref[:, pl.ds(first + h, 1), :] = jnp.broadcast_to(part[None], (parts_ref.shape[0], 1, LANES))


def weighted_sums(weighted_ref, block, w):
    acc = weighted_ref[block, strip(0)] * w[0:1, :]
    for s in range(1, w.shape[0]):
        acc = acc + weighted_ref[block, strip(s)] * w[s : s + 1, :]
    return acc


def spend_kernel(z_ref, reserve_ref, top_ref, weighted_ref, other_ref, pair_ref, parts_ref, scale_ref):
    rows, columns = weighted_ref.shape
    strips, halves = columns // LANES, rows // LANES
    lse = total_lse(z_ref, reserve_ref)
    spread_rows(scale_ref, pair_ref[0, pl.ds(strips, halves), :])
    put_parts(parts_ref, 0, weighted_sums(weighted_ref, pl.ds(0, rows), jnp.exp2(top_ref[...] - lse)))
    acc = jnp.zeros((rows, LANES), jnp.float32)
    for s in range(strips):
        y = other_ref[:, strip(s)] * scale_ref[...]
        acc = acc + y * jnp.exp2(y - lse[s : s + 1, :])
    put_parts(parts_ref, halves, acc)


def last_spend_kernel(z_ref, reserve_ref, top_ref, weighted_ref, parts_ref, prices_ref):
    rows = weighted_ref.shape[0] // 2
    lse = total_lse(z_ref, reserve_ref)
    prices_ref[...] = BACK * lse
    for k in range(2):
        w = jnp.exp2(top_ref[k] - lse)
        put_parts(parts_ref, k * (rows // LANES), weighted_sums(weighted_ref, pl.ds(k * rows, rows), w))


def pack_kernel(parts_ref, pace_ref, limits_ref, prices_ref, out_ref):
    strips, both = prices_ref.shape[0], pace_ref.shape[0]
    out_ref[pl.ds(0, strips), :] = prices_ref[...]
    out_ref[pl.ds(strips, both), :] = new_pace(parts_ref[...], pace_ref[...], limits_ref[...])
    out_ref[pl.ds(strips + both, 8 - both), :] = jnp.zeros((8 - both, LANES), jnp.float32)


def pick_kernel(pair_ref, pace_ref, prices_ref):
    strips, halves = prices_ref.shape[0], pace_ref.shape[0]
    prices_ref[...] = pair_ref[1, pl.ds(0, strips), :]
    second = lax.axis_index("adv") % CORES == 1
    mine = pair_ref[1, pl.ds(strips, halves), :]
    theirs = pair_ref[1, pl.ds(strips + halves, halves), :]
    pace_ref[...] = jnp.where(second, mine, theirs)


def f32(*shape):
    return jax.ShapeDtypeStruct(shape, jnp.float32)


def on_device(groups, values, limits, start_pace, reserve):
    rows, columns = values.shape
    imp = lax.axis_size("imp")
    far = lax.axis_size("adv") // NEAR
    strips, halves = columns // LANES, rows // LANES
    both = 2 * halves
    args = (values, start_pace.reshape(halves, LANES), limits.reshape(halves, LANES), reserve.reshape(strips, LANES))
    args = [pltpu.with_memory_space_constraint(a, pltpu.HBM) for a in args]

    def along_z(own):
        own = joined(lax.all_gather(own, "adv", axis_index_groups=groups["chips"]), far, strips, LANES)
        return lax.all_to_all(own, ("adv", "imp"), 0, 0, axis_index_groups=groups["z"], tiled=True)

    send, top, weighted, values, wide, reserve = pl.pallas_call(
        first_kernel,
        compiler_params=PARAMS,
        out_shape=(
            f32(strips + 2 * halves + 4, LANES),
            f32(strips, LANES),
            f32(rows, columns),
            jax.ShapeDtypeStruct((rows, columns), values.dtype),
            f32(rows, columns),
            f32(strips, LANES),
        ),
        in_specs=[HBM] * 4,
        out_specs=(VMEM,) * 6,
        scratch_shapes=[
            pltpu.VMEM((halves, LANES), jnp.float32),
            pltpu.VMEM((halves, LANES), jnp.float32),
            pltpu.VMEM((rows, LANES), jnp.float32),
            pltpu.SemaphoreType.DMA((CHUNKS + 3,)),
        ],
    )(*args)
    pair = lax.all_gather(send, "adv", axis_index_groups=groups["cores"])
    wide, pair = lax.optimization_barrier((wide, pair))
    other = lax.ppermute(wide, "adv", groups["ship"])
    parts = pl.pallas_call(
        spend_kernel,
        compiler_params=PARAMS,
        out_shape=f32(imp, both, LANES),
        in_specs=[VMEM] * 6,
        out_specs=VMEM,
        scratch_shapes=[pltpu.VMEM((rows, LANES), jnp.float32)],
    )(along_z(joined(pair, strips, LANES)), reserve, top, weighted, other, pair)
    parts = lax.all_to_all(parts, "imp", 0, 0, axis_index_groups=groups["imp"], tiled=True)
    pace, limits, own, top, weighted = pl.pallas_call(
        next_kernel,
        compiler_params=PARAMS,
        out_shape=(
            f32(both, LANES),
            f32(both, LANES),
            f32(strips, LANES),
            f32(2, strips, LANES),
            f32(2 * rows, columns),
        ),
        in_specs=[VMEM] * 5,
        out_specs=(VMEM,) * 5,
        scratch_shapes=[pltpu.VMEM((2 * rows, LANES), jnp.float32)],
    )(values, other, parts, send, pair)
    parts, prices = pl.pallas_call(
        last_spend_kernel,
        compiler_params=PARAMS,
        out_shape=(f32(imp, both, LANES), f32(strips, LANES)),
        in_specs=[VMEM] * 4,
        out_specs=(VMEM, VMEM),
    )(along_z(own), reserve, top, weighted)
    parts = lax.all_to_all(parts, "imp", 0, 0, axis_index_groups=groups["imp"], tiled=True)
    done = pl.pallas_call(
        pack_kernel,
        compiler_params=PARAMS,
        out_shape=f32(strips + 8, LANES),
        in_specs=[VMEM] * 4,
        out_specs=VMEM,
    )(parts, pace, limits, prices)
    pace, prices = pl.pallas_call(
        pick_kernel,
        compiler_params=PARAMS,
        out_shape=(f32(halves, LANES), f32(strips, LANES)),
        in_specs=[VMEM],
        out_specs=(VMEM, VMEM),
    )(lax.all_gather(done, "adv", axis_index_groups=groups["cores"]))
    return (pace.reshape(rows), prices.reshape(columns))


def solution(mesh):
    placed = (P("adv", "imp"), P("adv"), P("adv"), P("imp"))
    adv, imp = mesh.shape["adv"], mesh.shape["imp"]
    far, chips = adv // NEAR, NEAR // CORES

    def at(z, chip, core):
        return z * NEAR + chip * CORES + core

    order = ORDER_Z if far == len(ORDER_Z) else range(far)
    over_imp = ORDER_IMP if imp == len(ORDER_IMP) else range(imp)
    along_z = [[at(z, c, 1) * imp + i for z in order] for c in range(chips) for i in range(imp)]
    plane = [at(z, c, 0) * imp + i for z in range(far) for c in range(chips) for i in range(imp)]
    groups = dict(
        cores=[[at(z, c, k) for k in range(CORES)] for z in range(far) for c in range(chips)],
        chips=[[at(z, c, k) for c in range(chips)] for z in range(far) for k in range(CORES)],
        ship=[(at(z, c, 0), at(z, c, 1)) for z in range(far) for c in range(chips)],
        imp=[list(over_imp)],
        z=along_z + [plane[n : n + far] for n in range(0, len(plane), far)],
    )

    def step(*args):
        return on_device(groups, *args)

    return jax.shard_map(
        step, mesh=mesh, in_specs=placed, out_specs=(P("adv"), P("imp")), check_vma=False
    )
```
